32 devices in a mesh: row: 8 (over y, x, core), col: 4 (over z).
Axes of the slice: x: 2, y: 2, z: 4, core: 2. Of those that a mesh axis runs over, the one named last changes fastest.
Arguments:
- row_vectors: float32 [2048, 512], P('row', 'col'), may hold values from -0.05 to 0.05
- column_vectors: float32 [3072, 512], P(('col', 'row')), may hold values from -0.05 to 0.05
- occupation: float32 [512], replicated, may hold values from 0.1 to 4
- phi_row: float32 [32, 256, 256], P(('row', 'col')), may hold values from -6 to 6
- phi_col: float32 [32, 256, 1024], P(('row', 'col')), may hold values from -6 to 6
- potential: float32 [32, 256], P(('row', 'col')), may hold values from -6 to 6
- tile_owner: int32 [32, 8], P('row'), may hold values from 0 to 3, as said below
- tile_slot: int32 [32, 8], P('row'), may hold values from 0 to 5, as said below
- correlation: int32 [32, 8], P('row'), may hold values 0 or 1
Outputs:
- density: float32 [32, 256], P(('row', 'col'))
- potential_rows: float32 [32, 256], P(('row', 'col'))
The draws below stay inside these ranges and needn't reach their ends.
Inputs may be any that keep to these rules, and one draw needn't show every extreme that they name: `tile_owner`: within a row, at most two entries name the same holder, and in every row some holder is named by two entries. `tile_slot`: entries of one row with the same holder name different positions, so a batch's tiles are distinct.
All inputs are finite; a program needn't handle non-finite values. No bound on the sum of `correlation` on one device may be relied on, other than what follows from the above.
Results may differ from the reference program's by a relative error of at most 0.0003.
Values sent between devices are 32-bit elements; how exact they have to be, the bound alone decides.
No kernel may reach another device: no remote copies, remote signals or barrier semaphores. Data moves between devices by JAX's collectives and lax.ppermute only.
A program may use at most 64 MiB of HBM per device.

```python
import math
import jax
import jax.numpy as jnp
from jax import lax

RB = 256
K = 512
TW = 128
TPD = 6
TB = 8
NPTS = 256
SR = 2048
SC = 3072
BATCHES = 32
N_ROW = 8
N_COL = 4


def block_lists(key):
    batch_rows = N_ROW * N_COL
    first_key = jax.random.fold_in(key, 11)
    second_key = jax.random.fold_in(key, 12)
    third_key = jax.random.fold_in(key, 13)
    holders = jnp.arange(N_COL, dtype=jnp.int32)
    scores = jax.random.randint(first_key, (batch_rows, N_COL), 0, 2 ** 20, dtype=jnp.int32) * N_COL + holders[None, :]
    ranking = jnp.argsort(scores, axis=1).astype(jnp.int32)
    choose = jnp.array([0, 0] + [1 + (entry - 2) % (N_COL - 1) for entry in range(2, TB)], dtype=jnp.int32)
    initial = ranking[:, choose]
    position_scores = jax.random.randint(second_key, (batch_rows, TB), 0, 2 ** 20, dtype=jnp.int32) * TB + jnp.arange(TB, dtype=jnp.int32)[None, :]
    shuffle = jnp.argsort(position_scores, axis=1).astype(jnp.int32)
    owners = jnp.take_along_axis(initial, shuffle, axis=1)
    same = owners[:, :, None] == owners[:, None, :]
    lower = jnp.arange(TB)[:, None] > jnp.arange(TB)[None, :]
    ranks = jnp.sum((same & lower[None, :, :]).astype(jnp.int32), axis=2)
    offsets = jax.random.randint(third_key, (batch_rows, N_COL), 0, TPD, dtype=jnp.int32)
    chosen_offsets = jnp.take_along_axis(offsets, owners, axis=1)
    slots = (chosen_offsets + ranks) % TPD
    return (owners.astype(jnp.int32), slots.astype(jnp.int32))


def draw_tile_owner(key, part):
    return block_lists(key)[0]


def draw_tile_slot(key, part):
    return block_lists(key)[1]


def touch_ends(drawn, rng, low, top_value):
    dims = drawn.shape
    place = [jax.random.randint(jax.random.fold_in(rng, axis), (), 0, dims[axis]) for axis in range(len(dims))]
    drawn = drawn.at[tuple(place)].set(low)
    longest = dims.index(max(dims))
    place[longest] = (place[longest] + 1) % dims[longest]
    return drawn.at[tuple(place)].set(top_value)


def steps_of(own_key, extent, cuts, low, high):
    def one(axis_at, parts):
        draws = jax.random.uniform(jax.random.fold_in(jax.random.fold_in(own_key, 6), axis_at), (parts,), jnp.float32, low / len(cuts), high / len(cuts))
        return jnp.repeat(jnp.exp(draws), extent[axis_at] // parts).reshape((-1,) + (1,) * (len(extent) - axis_at - 1))

    gain = one(*cuts[0])
    for cut in cuts[1:]:
        gain = gain * one(*cut)
    return gain


def scatter_about(own_key, extent, deviation, reach, cuts=(), kind=jnp.bfloat16):
    values = jax.random.normal(own_key, extent, jnp.float32) * deviation
    if len(cuts) > 0:
        values = steps_of(own_key, extent, cuts, -0.22, 0.18) * values
    return jnp.clip(values, min=-reach, max=reach).astype(kind)


def setup_inputs(seed: int = 0) -> dict:
    key_list = jax.random.split(jax.random.key(seed), 10)
    row_vectors = scatter_about(key_list[0], (SR, K), 0.0078125, 0.05, ((0, 8), (1, 4)), jnp.float32)
    column_vectors = scatter_about(key_list[1], (SC, K), 0.0078125, 0.05, ((0, 32),), jnp.float32)
    occupation = jnp.clip(jnp.exp(jax.random.uniform(key_list[2], (K,), jnp.float32, math.log(0.1), math.log(4.0))), 0.1, 4.0)
    phi_row = scatter_about(key_list[3], (BATCHES, NPTS, RB), 1.0, 6.0, ((0, 32),), jnp.float32)
    phi_col = scatter_about(key_list[4], (BATCHES, NPTS, TB * TW), 1.0, 6.0, ((0, 32),), jnp.float32)
    potential = scatter_about(key_list[5], (BATCHES, NPTS), 1.0, 6.0, ((0, 32),), jnp.float32)
    tile_owner = draw_tile_owner(jax.random.fold_in(key_list[9], 71), 0)
    tile_slot = draw_tile_slot(jax.random.fold_in(key_list[9], 71), 0)
    correlation = touch_ends((jax.random.randint(key_list[8], (BATCHES, TB), 0, 4) < 3).astype(jnp.int32), jax.random.fold_in(key_list[8], 1), 0, 1)
    return {"row_vectors": row_vectors, "column_vectors": column_vectors, "occupation": occupation, "phi_row": phi_row, "phi_col": phi_col, "potential": potential, "tile_owner": tile_owner, "tile_slot": tile_slot, "correlation": correlation}


def reference(row_vectors, column_vectors, occupation, phi_row, phi_col, potential, tile_owner, tile_slot, correlation):
    batches = phi_row.shape[0]
    column_block = TPD * TW

    def one_batch(batch):
        block_row = batch // N_COL
        rows_needed = lax.dynamic_slice_in_dim(row_vectors, (block_row * RB).astype(jnp.int32), RB, 0)
        scaled = rows_needed * occupation[None, :]
        starts = tile_owner[batch] * column_block + tile_slot[batch] * TW
        indices = (starts[:, None] + jnp.arange(TW, dtype=jnp.int32)[None, :]).reshape(-1).astype(jnp.int32)
        columns = jnp.take(column_vectors, indices, axis=0)
        strips = lax.dot_general(scaled, columns, (((1,), (1,)), ((), ())),
                                 precision=lax.Precision.HIGHEST, preferred_element_type=jnp.float32)
        strips = strips.reshape(RB, TB, TW) * correlation[batch].astype(jnp.float32)[None, :, None]
        columns_field = phi_col[batch].reshape(NPTS, TB, TW)
        coupled = jnp.einsum("mkn,pkn->pm", strips, columns_field,
                             precision=lax.Precision.HIGHEST, preferred_element_type=jnp.float32)
        rows_field = phi_row[batch]
        density = jnp.sum(rows_field * coupled, axis=1)
        weighted = jnp.sum(potential[batch][:, None] * rows_field * coupled, axis=0)
        return density, weighted

    density, potential_rows = lax.map(one_batch, jnp.arange(batches, dtype=jnp.int32))
    return density, potential_rows
```

```python
import functools

import jax
import jax.numpy as jnp
from jax import lax
from jax.experimental import pallas as pl
from jax.experimental.pallas import tpu as pltpu
from jax.sharding import PartitionSpec as P

TW = 128
PAIR = 2
NT = (((1,), (1,)), ((), ()))
VMEM = pl.BlockSpec(memory_space=pltpu.VMEM)
SMEM = pl.BlockSpec(memory_space=pltpu.SMEM)


def split(x):
    high = x.astype(jnp.bfloat16)
    return high, (x - high.astype(jnp.float32)).astype(jnp.bfloat16)


def dot3(a, b):
    (ah, al), (bh, bl) = a, b
    one = functools.partial(
        lax.dot_general, dimension_numbers=NT, preferred_element_type=jnp.float32
    )
    return one(ah, bh) + (one(ah, bl) + one(al, bh))


def flip(x, axis, bit):
    size = lax.axis_size(axis)
    return lax.ppermute(x, axis, [(i, i ^ bit) for i in range(size)])


def gather_by_flips(x, axis):
    pieces = {0: x}
    bit = lax.axis_size(axis) // 2
    while bit:
        pieces.update({k ^ bit: flip(v, axis, bit) for k, v in list(pieces.items())})
        bit //= 2
    return [pieces[k] for k in range(len(pieces))]


def gather_columns(x):
    size = lax.axis_size("row")
    if size != 8:
        return [lax.all_gather(x, "row", axis=0, tiled=True)], None
    pieces = {0: x}
    for far in (2, 4, 6):
        pieces[far] = flip(x, "row", far)
    for near in (0, 2, 4, 6):
        pieces[near ^ 1] = flip(pieces[near], "row", 1)
    return [pieces[k] for k in range(8)], list(range(8))


def requests(owner_ref, values_ref, batch, holder):
    found = [jnp.int32(0)] * PAIR
    count = jnp.int32(0)
    for t in range(owner_ref.shape[1]):
        hit = owner_ref[batch, t] == holder
        value = values_ref[batch, t] if values_ref is not None else jnp.int32(t)
        for k in range(PAIR):
            found[k] = jnp.where(hit & (count == k), value, found[k])
        count = count + hit.astype(jnp.int32)
    return found, count


def density_kernel(groups, flips, n_chunks, *refs):
    owner_ref, slot_ref, occ_ref = refs[:3]
    row_refs = refs[3 : 3 + groups]
    chunk_refs = refs[3 + groups : 3 + groups + n_chunks]
    outs = refs[3 + groups + n_chunks : 3 + 2 * groups + n_chunks]
    scaled_ref, col_hi, col_lo = refs[3 + 2 * groups + n_chunks :]
    row, col = lax.axis_index("row"), lax.axis_index("col")
    quarter = row_refs[0].shape[1]
    for k in range(groups):
        source = col ^ k
        scaled_ref[source] = row_refs[k][...] * occ_ref[source]
    for k in range(n_chunks):
        size = chunk_refs[k].shape[0]
        place = pl.ds(0, size)
        if flips is not None:
            place = pl.ds(pl.multiple_of((row ^ flips[k]) * size, 32), size)
        col_hi[place, :], col_lo[place, :] = split(chunk_refs[k][...])
    scaled = jnp.concatenate([scaled_ref[k] for k in range(groups)], axis=1)
    left = split(scaled)
    for k in range(groups):
        slots, _ = requests(owner_ref, slot_ref, col ^ k, col)
        for j in range(PAIR):
            tile = pl.ds(pl.multiple_of(slots[j] * TW, TW), TW)
            outs[k][:, j * TW : (j + 1) * TW] = dot3(left, (col_hi[tile, :], col_lo[tile, :]))


def couple(owner_ref, corr_ref, phi_ref, strip, col, holder):
    places, count = requests(owner_ref, None, col, holder)
    parts = []
    for j in range(PAIR):
        weight = jnp.where(count > j, corr_ref[col, places[j]], 0).astype(jnp.float32)
        parts.append(phi_ref[0, :, pl.ds(pl.multiple_of(places[j] * TW, TW), TW)] * weight)
    return dot3(split(jnp.concatenate(parts, axis=1)), split(strip))


def own_kernel(owner_ref, corr_ref, phi_ref, strip_ref, out_ref):
    col = lax.axis_index("col")
    out_ref[...] = couple(owner_ref, corr_ref, phi_ref, strip_ref[...], col, col)


def final_kernel(groups, *refs):
    owner_ref, corr_ref, phi_ref, rows_ref, pot_ref, own_ref = refs[:6]
    strips = refs[6 : 5 + groups]
    density_ref, potential_ref = refs[5 + groups :]
    col = lax.axis_index("col")
    coupled = own_ref[...]
    for k in range(1, groups):
        coupled += couple(owner_ref, corr_ref, phi_ref, strips[k - 1][...], col, col ^ k)
    field = rows_ref[0] * coupled
    points = field.shape[0]
    ones = jnp.ones((8, field.shape[1]), jnp.float32)
    density_ref[...] = lax.dot_general(
        ones, field, NT, precision=lax.Precision.HIGHEST, preferred_element_type=jnp.float32
    )[:1]
    weights = jnp.broadcast_to(pot_ref[...], (8, points))
    potential_ref[...] = jnp.dot(
        weights, field, precision=lax.Precision.HIGHEST, preferred_element_type=jnp.float32
    )[:1]


def per_device(
    row_vectors,
    column_vectors,
    occupation,
    phi_row,
    phi_col,
    potential,
    tile_owner,
    tile_slot,
    correlation,
):
    groups = lax.axis_size("col")
    rows, quarter = row_vectors.shape
    states = occupation.shape[0]
    points = phi_col.shape[1]
    width = PAIR * TW
    chunks, flips = gather_columns(column_vectors)
    row_pieces = gather_by_flips(row_vectors, "col")
    block = sum(c.shape[0] for c in chunks)
    strips = pl.pallas_call(
        functools.partial(density_kernel, groups, flips, len(chunks)),
        out_shape=[jax.ShapeDtypeStruct((rows, width), jnp.float32)] * groups,
        in_specs=[SMEM, SMEM] + [VMEM] * (1 + groups + len(chunks)),
        out_specs=[VMEM] * groups,
        scratch_shapes=[
            pltpu.VMEM((groups, rows, quarter), jnp.float32),
            pltpu.VMEM((block, states), jnp.bfloat16),
            pltpu.VMEM((block, states), jnp.bfloat16),
        ],
        name="density",
    )(
        tile_owner,
        tile_slot,
        occupation.reshape(groups, 1, quarter),
        *row_pieces,
        *chunks,
    )
    arrived = [flip(strips[k], "col", k) for k in range(1, groups)]
    own = pl.pallas_call(
        own_kernel,
        out_shape=jax.ShapeDtypeStruct((points, rows), jnp.float32),
        in_specs=[SMEM, SMEM, VMEM, VMEM],
        out_specs=VMEM,
        name="own",
        cost_estimate=pl.CostEstimate(
            flops=2 * points * rows * width * 3, bytes_accessed=2 << 20, transcendentals=0
        ),
    )(tile_owner, correlation, phi_col, strips[0])
    return tuple(
        pl.pallas_call(
            functools.partial(final_kernel, groups),
            out_shape=[
                jax.ShapeDtypeStruct((1, points), jnp.float32),
                jax.ShapeDtypeStruct((1, rows), jnp.float32),
            ],
            in_specs=[SMEM, SMEM] + [VMEM] * (4 + groups - 1),
            out_specs=[VMEM, VMEM],
            name="final",
        )(tile_owner, correlation, phi_col, phi_row, potential, own, *arrived)
    )


def solution(mesh):
    in_specs = (
        P("row", "col"),
        P(("col", "row"), None),
        P(),
        P(("row", "col"), None, None),
        P(("row", "col"), None, None),
        P(("row", "col"), None),
        P("row", None),
        P("row", None),
        P("row", None),
    )
    out_specs = (P(("row", "col"), None), P(("row", "col"), None))
    return jax.shard_map(
        per_device, mesh=mesh, in_specs=in_specs, out_specs=out_specs, check_vma=False
    )
```

```python
import functools

import jax
import jax.numpy as jnp
from jax import lax
from jax.experimental import pallas as pl
from jax.experimental.pallas import tpu as pltpu
from jax.sharding import PartitionSpec as P


TW = 128
PAIR = 2
NT = (((1,), (1,)), ((), ()))
PARAMS = pltpu.CompilerParams(vmem_limit_bytes=16 << 20)
VMEM = pl.BlockSpec(memory_space=pltpu.VMEM)
HBM = pl.BlockSpec(memory_space=pltpu.HBM)
SMEM = pl.BlockSpec(memory_space=pltpu.SMEM)


def split(x):
    high = x.astype(jnp.bfloat16)
    return high, (x - high.astype(jnp.float32)).astype(jnp.bfloat16)


def dot3(a, b):
    (ah, al), (bh, bl) = a, b
    one = functools.partial(
        lax.dot_general, dimension_numbers=NT, preferred_element_type=jnp.float32
    )
    return one(ah, bh) + (one(ah, bl) + one(al, bh))


def flip(x, axis, bit):
    size = lax.axis_size(axis)
    return lax.ppermute(x, axis, [(i, i ^ bit) for i in range(size)])


def gather_rows(x):
    pieces = {0: x}
    bit = lax.axis_size("col") // 2
    while bit:
        for k, v in list(pieces.items()):
            pieces[k ^ bit] = flip(v, "col", bit)
        bit //= 2
    return [pieces[k] for k in range(len(pieces))]


def gather_columns(x):
    if lax.axis_size("row") != 8:
        return [lax.all_gather(x, "row", axis=0, tiled=True)]
    pieces = {0: x}
    for far in (2, 4, 6):
        pieces[far] = flip(x, "row", far)
    for near in (0, 2, 4, 6):
        pieces[near ^ 1] = flip(pieces[near], "row", 1)
    return [pieces[k] for k in range(8)]


def place(row, pieces, k):
    size = pieces[k].shape[0]
    if len(pieces) == 1:
        return pl.ds(0, size)
    return pl.ds(pl.multiple_of((row ^ k) * size, 32), size)


def requests(owner_ref, values_ref, batch, holder):
    found = [jnp.int32(0)] * PAIR
    count = jnp.int32(0)
    for t in range(owner_ref.shape[1]):
        hit = owner_ref[batch, t] == holder
        value = values_ref[batch, t] if values_ref is not None else jnp.int32(t)
        for k in range(PAIR):
            found[k] = jnp.where(hit & (count == k), value, found[k])
        count = count + hit.astype(jnp.int32)
    return found, count


def tile(ref, slot):
    return ref[pl.ds(pl.multiple_of(slot * TW, TW), TW), :]


def prepare_kernel(served, far, *refs):
    sources, refs = refs[:8], refs[8:]
    slots_out, row_out, hi_out, lo_out, occ_ref, phi_hi, phi_lo, pot_out = refs[:8]
    owner_ref, slot_ref, corr_ref, row_ref, chunk_ref, phi_ref, pot_ref, sems = refs[8:]
    targets = owner_ref, slot_ref, corr_ref, row_ref, chunk_ref, occ_ref, phi_ref, pot_ref
    copies = [
        pltpu.make_async_copy(source, target, sems.at[i])
        for i, (source, target) in enumerate(zip(sources, targets))
    ]
    for copy in copies:
        copy.start()
    for copy in copies:
        copy.wait()
    col = lax.axis_index("col")
    for i, k in enumerate(served):
        slots, _ = requests(owner_ref, slot_ref, col ^ k, col)
        for j in range(PAIR):
            slots_out[i * PAIR + j] = slots[j]
    slots, _ = requests(owner_ref, slot_ref, col, col ^ far)
    for j in range(PAIR):
        slots_out[len(served) * PAIR + j] = slots[j]
    row_out[...] = row_ref[...] * occ_ref[col]
    pot_out[...] = jnp.broadcast_to(pot_ref[...], (TW, pot_ref.shape[1])).T
    hi_out[...], lo_out[...] = split(chunk_ref[...])
    for k in range(phi_hi.shape[0]):
        places, count = requests(owner_ref, None, col, col ^ k)
        for j in range(PAIR):
            weight = jnp.where(count > j, corr_ref[col, places[j]], 0).astype(jnp.float32)
            part = phi_ref[0, :, pl.ds(pl.multiple_of(places[j] * TW, TW), TW)] * weight
            at = slice(j * TW, (j + 1) * TW)
            phi_hi[k, :, at], phi_lo[k, :, at] = split(part)


def tiles(refs, slots_ref, i):
    return [
        jnp.concatenate([tile(ref, slots_ref[i * PAIR + j]) for j in range(PAIR)], axis=0)
        for ref in refs
    ]


def density_kernel(groups, n_served, n_chunks, *refs):
    slots_ref, own_row, own_hi, own_lo, occ_ref = refs[:5]
    refs = refs[5:]
    row_refs, chunk_refs = refs[: groups - 1], refs[groups - 1 : groups - 1 + n_chunks]
    refs = refs[groups - 1 + n_chunks :]
    scaled_hi, scaled_lo = refs[:2]
    outs = refs[2 : 2 + n_served]
    scaled_ref, col_hi, col_lo = refs[2 + n_served :]
    row, col = lax.axis_index("row"), lax.axis_index("col")
    for k in range(n_chunks):
        at = place(row, chunk_refs, k)
        if k == 0 and n_chunks > 1:
            col_hi[at, :], col_lo[at, :] = own_hi[...], own_lo[...]
        else:
            col_hi[at, :], col_lo[at, :] = split(chunk_refs[k][...])
    scaled_ref[col] = own_row[...]
    for k in range(1, groups):
        scaled_ref[col ^ k] = row_refs[k - 1][...] * occ_ref[col ^ k]
    left = split(jnp.concatenate([scaled_ref[k] for k in range(groups)], axis=1))
    scaled_hi[...], scaled_lo[...] = left
    for i, out in enumerate(outs):
        out[...] = dot3(left, tiles((col_hi, col_lo), slots_ref, i))


def own_kernel(phi_hi, phi_lo, strip_ref, out_ref):
    out_ref[...] = dot3((phi_hi[0], phi_lo[0]), split(strip_ref[...]))


def final_kernel(far, others, n_chunks, *refs):
    slots_ref, phi_hi, phi_lo, rows_ref, pot_ref, own_ref, hi_ref, lo_ref = refs[:8]
    chunks, refs = refs[8 : 8 + n_chunks], refs[8 + n_chunks :]
    strips, (density_ref, potential_ref, block_ref) = refs[: len(others)], refs[len(others) :]
    row = lax.axis_index("row")
    for k in range(n_chunks):
        block_ref[place(row, chunks, k), :] = chunks[k][...]
    columns = tiles((block_ref,), slots_ref, len(others) + 1)[0]
    strip = dot3((hi_ref[...], lo_ref[...]), split(columns))
    coupled = own_ref[...] + dot3((phi_hi[far], phi_lo[far]), split(strip))
    for k, strip_ref in zip(others, strips):
        coupled += dot3((phi_hi[k], phi_lo[k]), split(strip_ref[...]))
    field = rows_ref[0] * coupled
    weights = pot_ref[...]
    parts = [field[:, at : at + TW] for at in range(0, field.shape[1], TW)]
    for at, part in enumerate(parts):
        potential_ref[:, at * TW : (at + 1) * TW] = jnp.sum(part * weights, axis=0, keepdims=True)
    ones = jnp.ones((8, TW), jnp.bfloat16)
    density_ref[...] = sum(
        lax.dot_general(ones, part, NT, preferred_element_type=jnp.float32)
        for part in split(sum(parts))
    )[:1]


def call(kernel, in_specs, outs, scratch=(), flops=0):
    out_specs = [SMEM if len(o.shape) == 1 else VMEM for o in outs]
    return pl.pallas_call(
        kernel,
        out_shape=outs,
        in_specs=in_specs,
        out_specs=out_specs,
        scratch_shapes=list(scratch),
        compiler_params=PARAMS,
        cost_estimate=pl.CostEstimate(flops=flops, bytes_accessed=2 << 20, transcendentals=0),
    )


def per_device(
    row_vectors,
    column_vectors,
    occupation,
    phi_row,
    phi_col,
    potential,
    tile_owner,
    tile_slot,
    correlation,
):
    groups = lax.axis_size("col")
    rows, quarter = row_vectors.shape
    states = occupation.shape[0]
    points = phi_col.shape[1]
    width = PAIR * TW
    block = column_vectors.shape[0] * lax.axis_size("row")
    far = groups // 2
    others = [k for k in range(groups - 1, 0, -1) if k != far]
    served = others + [0]
    f32 = lambda *shape: jax.ShapeDtypeStruct(shape, jnp.float32)
    bf16 = lambda *shape: jax.ShapeDtypeStruct(shape, jnp.bfloat16)
    row_pieces = gather_rows(row_vectors)
    chunks = gather_columns(column_vectors)
    crossed = flip(column_vectors, "col", far)
    far_chunks = gather_columns(crossed)
    slots, own_row, own_hi, own_lo, occ, phi_hi, phi_lo, pot = call(
        functools.partial(prepare_kernel, served, far),
        [HBM] * 8,
        [
            jax.ShapeDtypeStruct(((len(served) + 1) * PAIR,), jnp.int32),
            f32(rows, quarter),
            bf16(*column_vectors.shape),
            bf16(*column_vectors.shape),
            f32(groups, 1, quarter),
            bf16(groups, points, width),
            bf16(groups, points, width),
            f32(points, TW),
        ],
        [pltpu.SMEM(tile_owner.shape, jnp.int32)] * 3
        + [pltpu.VMEM(a.shape, jnp.float32) for a in (row_vectors, column_vectors, phi_col, potential)]
        + [pltpu.SemaphoreType.DMA((8,))],
    )(
        *(
            pltpu.with_memory_space_constraint(a, pltpu.HBM)
            for a in (
                tile_owner,
                tile_slot,
                correlation,
                row_vectors,
                column_vectors,
                occupation.reshape(groups, 1, quarter),
                phi_col,
                potential,
            )
        )
    )
    if len(chunks) > 1:
        chunks[0] = own_hi
    scaled_hi, scaled_lo, *strips = call(
        functools.partial(density_kernel, groups, len(served), len(chunks)),
        [SMEM] + [VMEM] * (3 + groups + len(chunks)),
        [bf16(rows, states)] * 2 + [f32(rows, width)] * len(served),
        [
            pltpu.VMEM((groups, rows, quarter), jnp.float32),
            pltpu.VMEM((block, states), jnp.bfloat16),
            pltpu.VMEM((block, states), jnp.bfloat16),
        ],
        6 * rows * width * states * len(served),
    )(slots, own_row, own_hi, own_lo, occ, *row_pieces[1:], *chunks)
    strips = dict(zip(served, strips))
    arrived = [flip(strips[k], "col", k) for k in others]
    own = call(own_kernel, [VMEM] * 3, [f32(points, rows)], (), 6 * points * rows * width)(
        phi_hi, phi_lo, strips[0]
    )[0]
    return tuple(
        call(
            functools.partial(final_kernel, far, others, len(far_chunks)),
            [SMEM] + [VMEM] * (7 + len(far_chunks) + len(others)),
            [f32(1, points), f32(1, rows)],
            [pltpu.VMEM((block, states), jnp.float32)],
        )(slots, phi_hi, phi_lo, phi_row, pot, own, scaled_hi, scaled_lo, *far_chunks, *arrived)
    )


def solution(mesh):
    in_specs = (
        P("row", "col"),
        P(("col", "row"), None),
        P(),
        P(("row", "col"), None, None),
        P(("row", "col"), None, None),
        P(("row", "col"), None),
        P("row", None),
        P("row", None),
        P("row", None),
    )
    out_specs = (P(("row", "col"), None), P(("row", "col"), None))

    return jax.shard_map(
        per_device, mesh=mesh, in_specs=in_specs, out_specs=out_specs, check_vma=False
    )
```

```python
import functools

import jax
import jax.numpy as jnp
from jax import lax
from jax.experimental import pallas as pl
from jax.experimental.pallas import tpu as pltpu
from jax.sharding import PartitionSpec as P


TW = 128
PAIR = 2
NT = (((1,), (1,)), ((), ()))
PARAMS = pltpu.CompilerParams(vmem_limit_bytes=16 << 20)
VMEM = pl.BlockSpec(memory_space=pltpu.VMEM)
HBM = pl.BlockSpec(memory_space=pltpu.HBM)
SMEM = pl.BlockSpec(memory_space=pltpu.SMEM)


def split(x):
    high = x.astype(jnp.bfloat16)
    return high, (x - high.astype(jnp.float32)).astype(jnp.bfloat16)


def dot3(a, b):
    (ah, al), (bh, bl) = a, b
    one = functools.partial(
        lax.dot_general, dimension_numbers=NT, preferred_element_type=jnp.float32
    )
    return one(ah, bh) + (one(ah, bl) + one(al, bh))


def flip(x, axis, bit):
    size = lax.axis_size(axis)
    return lax.ppermute(x, axis, [(i, i ^ bit) for i in range(size)])


def gather_rows(x):
    pieces = {0: x}
    bit = lax.axis_size("col") // 2
    while bit:
        for k, v in list(pieces.items()):
            pieces[k ^ bit] = flip(v, "col", bit)
        bit //= 2
    return [pieces[k] for k in range(len(pieces))]


def gather_columns(x):
    if lax.axis_size("row") != 8:
        return [lax.all_gather(x, "row", axis=0, tiled=True)]
    pieces = {0: x}
    for far in (2, 4, 6):
        pieces[far] = flip(x, "row", far)
    for near in (0, 2, 4, 6):
        pieces[near ^ 1] = flip(pieces[near], "row", 1)
    return [pieces[k] for k in range(8)]


def place(row, k, pieces):
    size = pieces[k].shape[0]
    if len(pieces) == 1:
        return pl.ds(0, size)
    return pl.ds(pl.multiple_of((row ^ k) * size, 16), size)


def requests(owner_ref, values_ref, batch, holder):
    found = [jnp.int32(0)] * PAIR
    count = jnp.int32(0)
    for t in range(owner_ref.shape[1]):
        hit = owner_ref[batch, t] == holder
        value = values_ref[batch, t] if values_ref is not None else jnp.int32(t)
        for k in range(PAIR):
            found[k] = jnp.where(hit & (count == k), value, found[k])
        count = count + hit.astype(jnp.int32)
    return found, count


def tile(ref, slot):
    return ref[pl.ds(pl.multiple_of(slot * TW, TW), TW), :]


def start_copies(sources, targets, sems):
    copies = [
        pltpu.make_async_copy(source, target, sems.at[i])
        for i, (source, target) in enumerate(zip(sources, targets))
    ]
    for copy in copies:
        copy.start()
    return copies


def basis_kernel(*refs):
    sources, refs = refs[:5], refs[5:]
    phi_hi, phi_lo, pot_out, rows_out, owner_ref, corr_ref, phi_ref, pot_ref, sems = refs
    targets = owner_ref, corr_ref, phi_ref, pot_ref, rows_out
    copies = start_copies(sources, targets, sems)
    for copy in copies[:-1]:
        copy.wait()
    col = lax.axis_index("col")
    pot_out[...] = jnp.broadcast_to(pot_ref[...], (TW, pot_ref.shape[1])).T
    for k in range(phi_hi.shape[0]):
        places, count = requests(owner_ref, None, col, col ^ k)
        for j in range(PAIR):
            weight = jnp.where(count > j, corr_ref[col, places[j]], 0).astype(jnp.float32)
            part = phi_ref[0, :, pl.ds(pl.multiple_of(places[j] * TW, TW), TW)] * weight
            at = slice(j * TW, (j + 1) * TW)
            phi_hi[k, :, at], phi_lo[k, :, at] = split(part)
    copies[-1].wait()


def tiles(refs, slots_ref, i):
    return [
        jnp.concatenate([tile(ref, slots_ref[i * PAIR + j]) for j in range(PAIR)], axis=0)
        for ref in refs
    ]


def tables_kernel(served, far, *refs):
    sources, refs = refs[:5], refs[5:]
    slots_ref, occ_ref, own_row, own_hi, own_lo = refs[:5]
    row_ref, chunk_ref, owner_ref, slot_ref, sems = refs[5:]
    targets = owner_ref, slot_ref, occ_ref, row_ref, chunk_ref
    for copy in start_copies(sources, targets, sems):
        copy.wait()
    col = lax.axis_index("col")
    for i, k in enumerate(served):
        slots, _ = requests(owner_ref, slot_ref, col ^ k, col)
        for j in range(PAIR):
            slots_ref[i * PAIR + j] = slots[j]
    slots, _ = requests(owner_ref, slot_ref, col, col ^ far)
    for j in range(PAIR):
        slots_ref[len(served) * PAIR + j] = slots[j]
    own_hi[...], own_lo[...] = split(chunk_ref[...])
    own_row[...] = row_ref[...] * occ_ref[col]


def early_kernel(groups, n_served, n_chunks, slots_ref, occ_ref, own_row, own_hi, own_lo, *refs):
    row_refs, refs = refs[: groups - 2], refs[groups - 2 :]
    chunk_refs, refs = refs[:n_chunks], refs[n_chunks:]
    left_hi, left_lo, partial_ref, last_hi, last_lo, scaled_ref, col_hi, col_lo = refs
    row, col = lax.axis_index("row"), lax.axis_index("col")
    last = col ^ (groups - 1)
    for k in range(n_chunks):
        at = place(row, k, chunk_refs)
        if k == 0 and n_chunks > 1:
            col_hi[at, :], col_lo[at, :] = own_hi[...], own_lo[...]
        else:
            col_hi[at, :], col_lo[at, :] = split(chunk_refs[k][...])
    scaled_ref[col] = own_row[...]
    for k in range(1, groups - 1):
        scaled_ref[col ^ k] = row_refs[k - 1][...] * occ_ref[col ^ k]
    scaled_ref[last] = jnp.zeros_like(own_row)
    left = split(jnp.concatenate([scaled_ref[k] for k in range(groups)], axis=1))
    left_hi[...], left_lo[...] = left
    quarter = last_hi.shape[2]
    for i in range(n_served):
        right = tiles((col_hi, col_lo), slots_ref, i)
        partial_ref[i] = dot3(left, right)
        for out, side in zip((last_hi, last_lo), right):
            out[i] = pick(side, last, quarter)


def pick(x, index, size):
    out = x[:, :size]
    for k in range(1, x.shape[1] // size):
        out = jnp.where(index == k, x[:, k * size : (k + 1) * size], out)
    return out


def density_kernel(groups, row_ref, occ_ref, partial_ref, right_hi, right_lo, *outs):
    row_hi, row_lo = outs[:2]
    left = split(row_ref[...] * occ_ref[lax.axis_index("col") ^ (groups - 1)])
    row_hi[...], row_lo[...] = left
    for i, out in enumerate(outs[2:]):
        out[...] = partial_ref[i] + dot3(left, (right_hi[i], right_lo[i]))


def own_kernel(groups, phi_hi, phi_lo, strip_ref, left_hi, left_lo, row_hi, row_lo, *outs):
    out_ref, full_hi, full_lo = outs
    out_ref[...] = dot3((phi_hi[0], phi_lo[0]), split(strip_ref[...]))
    last = lax.axis_index("col") ^ (groups - 1)
    quarter = row_hi.shape[1]
    for full, left, row in ((full_hi, left_hi, row_hi), (full_lo, left_lo, row_lo)):
        full[...] = jnp.concatenate(
            [
                jnp.where(last == k, row[...], left[:, k * quarter : (k + 1) * quarter])
                for k in range(groups)
            ],
            axis=1,
        )


def strips_kernel(others, phi_hi, phi_lo, own_ref, *refs):
    total = own_ref[...]
    for k, strip_ref in zip(others, refs):
        total += dot3((phi_hi[k], phi_lo[k]), split(strip_ref[...]))
    refs[-1][...] = total


def final_kernel(far, index, n_chunks, *refs):
    slots_ref, phi_hi, phi_lo, rows_ref, pot_ref, sum_ref, left_hi, left_lo = refs[:8]
    chunks, (density_ref, potential_ref, block_ref) = refs[8 : 8 + n_chunks], refs[8 + n_chunks :]
    row = lax.axis_index("row")
    for k in range(n_chunks):
        block_ref[place(row, k, chunks), :] = chunks[k][...]
    columns = tiles((block_ref,), slots_ref, index)[0]
    strip = dot3((left_hi[...], left_lo[...]), split(columns))
    coupled = sum_ref[...] + dot3((phi_hi[far], phi_lo[far]), split(strip))
    field = rows_ref[0] * coupled
    weights = pot_ref[...]
    parts = [field[:, at : at + TW] for at in range(0, field.shape[1], TW)]
    for at, part in enumerate(parts):
        potential_ref[:, at * TW : (at + 1) * TW] = jnp.sum(part * weights, axis=0, keepdims=True)
    ones = jnp.ones((8, TW), jnp.bfloat16)
    density_ref[...] = sum(
        lax.dot_general(ones, part, NT, preferred_element_type=jnp.float32)
        for part in split(sum(parts))
    )[:1]


def call(kernel, in_specs, outs, scratch=(), flops=0):
    out_specs = [SMEM if len(o.shape) == 1 else VMEM for o in outs]
    return pl.pallas_call(
        kernel,
        out_shape=outs,
        in_specs=in_specs,
        out_specs=out_specs,
        scratch_shapes=list(scratch),
        compiler_params=PARAMS,
        cost_estimate=pl.CostEstimate(flops=flops, bytes_accessed=2 << 20, transcendentals=0),
    )


def per_device(
    row_vectors,
    column_vectors,
    occupation,
    phi_row,
    phi_col,
    potential,
    tile_owner,
    tile_slot,
    correlation,
):
    groups = lax.axis_size("col")
    rows, quarter = row_vectors.shape
    states = occupation.shape[0]
    points = phi_col.shape[1]
    width = PAIR * TW
    block = column_vectors.shape[0] * lax.axis_size("row")
    far = groups // 2
    others = [k for k in range(groups - 1, 0, -1) if k != far]
    served = others + [0]
    f32 = lambda *shape: jax.ShapeDtypeStruct(shape, jnp.float32)
    bf16 = lambda *shape: jax.ShapeDtypeStruct(shape, jnp.bfloat16)
    row_pieces = gather_rows(row_vectors)
    chunks = gather_columns(column_vectors)
    far_chunks = gather_columns(flip(column_vectors, "col", far))
    n_served = len(served)
    in_hbm = lambda *arrays: [pltpu.with_memory_space_constraint(a, pltpu.HBM) for a in arrays]
    tables = [pltpu.SMEM(tile_owner.shape, jnp.int32)] * 2
    phi_hi, phi_lo, pot, rows_field = call(
        basis_kernel,
        [HBM] * 5,
        [bf16(groups, points, width)] * 2 + [f32(points, TW), f32(*phi_row.shape)],
        tables
        + [pltpu.VMEM(a.shape, jnp.float32) for a in (phi_col, potential)]
        + [pltpu.SemaphoreType.DMA((5,))],
    )(*in_hbm(tile_owner, correlation, phi_col, potential, phi_row))
    slots, occ, own_row, own_hi, own_lo = call(
        functools.partial(tables_kernel, served, far),
        [HBM] * 5,
        [
            jax.ShapeDtypeStruct(((n_served + 1) * PAIR,), jnp.int32),
            f32(groups, 1, quarter),
            f32(rows, quarter),
            *[bf16(*column_vectors.shape)] * 2,
        ],
        [
            pltpu.VMEM((rows, quarter), jnp.float32),
            pltpu.VMEM(column_vectors.shape, jnp.float32),
            *tables,
            pltpu.SemaphoreType.DMA((5,)),
        ],
    )(
        *in_hbm(
            tile_owner,
            tile_slot,
            occupation.reshape(groups, 1, quarter),
            row_vectors,
            column_vectors,
        )
    )
    if len(chunks) > 1:
        chunks[0] = own_hi
    left_hi, left_lo, partial, right_hi, right_lo = call(
        functools.partial(early_kernel, groups, n_served, len(chunks)),
        [SMEM] + [VMEM] * (4 + groups - 2 + len(chunks)),
        [
            *[bf16(rows, states)] * 2,
            f32(n_served, rows, width),
            *[bf16(n_served, width, quarter)] * 2,
        ],
        [
            pltpu.VMEM((groups, rows, quarter), jnp.float32),
            *[pltpu.VMEM((block, states), jnp.bfloat16)] * 2,
        ],
        6 * rows * width * states * n_served,
    )(slots, occ, own_row, own_hi, own_lo, *row_pieces[1:-1], *chunks)
    row_hi, row_lo, *strips = call(
        functools.partial(density_kernel, groups),
        [VMEM] * 5,
        [bf16(rows, quarter)] * 2 + [f32(rows, width)] * n_served,
        (),
        6 * rows * width * quarter * n_served,
    )(row_pieces[-1], occ, partial, right_hi, right_lo)
    strips = dict(zip(served, strips))
    arrived = [flip(strips[k], "col", k) for k in others]
    own, full_hi, full_lo = call(
        functools.partial(own_kernel, groups),
        [VMEM] * 7,
        [f32(points, rows)] + [bf16(rows, states)] * 2,
        (),
        6 * points * rows * width,
    )(phi_hi, phi_lo, strips[0], left_hi, left_lo, row_hi, row_lo)
    summed = call(
        functools.partial(strips_kernel, others),
        [VMEM] * (3 + len(others)),
        [f32(points, rows)],
        (),
        6 * points * rows * width * len(others),
    )(phi_hi, phi_lo, own, *arrived)[0]
    return tuple(
        call(
            functools.partial(final_kernel, far, n_served, len(far_chunks)),
            [SMEM] + [VMEM] * (7 + len(far_chunks)),
            [f32(1, points), f32(1, rows)],
            [pltpu.VMEM((block, states), jnp.float32)],
        )(slots, phi_hi, phi_lo, rows_field, pot, summed, full_hi, full_lo, *far_chunks)
    )


def solution(mesh):
    in_specs = (
        P("row", "col"),
        P(("col", "row"), None),
        P(),
        P(("row", "col"), None, None),
        P(("row", "col"), None, None),
        P(("row", "col"), None),
        P("row", None),
        P("row", None),
        P("row", None),
    )
    out_specs = (P(("row", "col"), None), P(("row", "col"), None))

    return jax.shard_map(
        per_device, mesh=mesh, in_specs=in_specs, out_specs=out_specs, check_vma=False
    )
```

```python
import functools

import jax
import jax.numpy as jnp
from jax import lax
from jax.experimental import pallas as pl
from jax.experimental.pallas import tpu as pltpu
from jax.sharding import PartitionSpec as P


TW = 128
PAIR = 2
NT = (((1,), (1,)), ((), ()))
PARAMS = pltpu.CompilerParams(vmem_limit_bytes=16 << 20)
VMEM = pl.BlockSpec(memory_space=pltpu.VMEM)
HBM = pl.BlockSpec(memory_space=pltpu.HBM)
SMEM = pl.BlockSpec(memory_space=pltpu.SMEM)


def split(x):
    high = x.astype(jnp.bfloat16)
    return high, (x - high.astype(jnp.float32)).astype(jnp.bfloat16)


def dot3(a, b):
    (ah, al), (bh, bl) = a, b
    one = functools.partial(
        lax.dot_general, dimension_numbers=NT, preferred_element_type=jnp.float32
    )
    return one(ah, bh) + (one(ah, bl) + one(al, bh))


def flip(x, axis, bit):
    size = lax.axis_size(axis)
    return lax.ppermute(x, axis, [(i, i ^ bit) for i in range(size)])


def gather_rows(x):
    pieces = {0: x}
    bit = lax.axis_size("col") // 2
    while bit:
        for k, v in list(pieces.items()):
            pieces[k ^ bit] = flip(v, "col", bit)
        bit //= 2
    return [pieces[k] for k in range(len(pieces))]


def gather_columns(x):
    if lax.axis_size("row") != 8:
        return [lax.all_gather(x, "row", axis=0, tiled=True)]
    pieces = {0: x}
    for far in (2, 4, 6):
        pieces[far] = flip(x, "row", far)
    for near in (0, 2, 4, 6):
        pieces[near ^ 1] = flip(pieces[near], "row", 1)
    return [pieces[k] for k in range(8)]


FIRST = (0, 1, 2, 4, 6)


def fill(row, count, ks, refs, high, low):
    for k, ref in zip(ks, refs):
        size = ref.shape[0]
        at = pl.ds(pl.multiple_of((row ^ k) * size, 16), size) if count > 1 else pl.ds(0, size)
        high[at, :], low[at, :] = split(ref[...])


def two(count):
    first = [k for k in FIRST if k < count]
    return first, [k for k in range(count) if k not in first]


def requests(owner_ref, values_ref, batch, holder):
    found = [jnp.int32(0)] * PAIR
    count = jnp.int32(0)
    for t in range(owner_ref.shape[1]):
        hit = owner_ref[batch, t] == holder
        value = values_ref[batch, t] if values_ref is not None else jnp.int32(t)
        for k in range(PAIR):
            found[k] = jnp.where(hit & (count == k), value, found[k])
        count = count + hit.astype(jnp.int32)
    return found, count


def tile(ref, slot):
    return ref[pl.ds(pl.multiple_of(slot * TW, TW), TW), :]


def start_copies(sources, targets, sems):
    copies = [
        pltpu.make_async_copy(source, target, sems.at[i])
        for i, (source, target) in enumerate(zip(sources, targets))
    ]
    for copy in copies:
        copy.start()
    return copies


def basis_kernel(*refs):
    sources, refs = refs[:5], refs[5:]
    phi_hi, phi_lo, pot_out, rows_out, owner_ref, corr_ref, phi_ref, pot_ref, sems = refs
    targets = owner_ref, corr_ref, phi_ref, pot_ref, rows_out
    copies = start_copies(sources, targets, sems)
    for copy in copies[:-1]:
        copy.wait()
    col = lax.axis_index("col")
    pot_out[...] = jnp.broadcast_to(pot_ref[...], (TW, pot_ref.shape[1])).T
    for k in range(phi_hi.shape[0]):
        places, count = requests(owner_ref, None, col, col ^ k)
        for j in range(PAIR):
            weight = jnp.where(count > j, corr_ref[col, places[j]], 0).astype(jnp.float32)
            part = phi_ref[0, :, pl.ds(pl.multiple_of(places[j] * TW, TW), TW)] * weight
            at = slice(j * TW, (j + 1) * TW)
            phi_hi[k, :, at], phi_lo[k, :, at] = split(part)
    copies[-1].wait()


def tiles(refs, slots_ref, i):
    return [
        jnp.concatenate([tile(ref, slots_ref[i * PAIR + j]) for j in range(PAIR)], axis=0)
        for ref in refs
    ]


def tables_kernel(served, far, *refs):
    sources, refs = refs[:5], refs[5:]
    slots_ref, occ_ref, own_row, chunk_ref = refs[:4]
    row_ref, owner_ref, slot_ref, sems = refs[4:]
    targets = owner_ref, slot_ref, occ_ref, row_ref, chunk_ref
    for copy in start_copies(sources, targets, sems):
        copy.wait()
    col = lax.axis_index("col")
    for i, k in enumerate(served):
        slots, _ = requests(owner_ref, slot_ref, col ^ k, col)
        for j in range(PAIR):
            slots_ref[i * PAIR + j] = slots[j]
    slots, _ = requests(owner_ref, slot_ref, col, col ^ far)
    for j in range(PAIR):
        slots_ref[len(served) * PAIR + j] = slots[j]
    own_row[...] = row_ref[...] * occ_ref[col]


def split_kernel(groups, count, occ_ref, own_row, *refs):
    row_refs, refs = refs[: groups - 2], refs[groups - 2 :]
    first, _ = two(count)
    chunk_refs, refs = refs[: len(first)], refs[len(first) :]
    left_hi, left_lo, col_hi, col_lo, scaled_ref = refs
    col = lax.axis_index("col")
    fill(lax.axis_index("row"), count, first, chunk_refs, col_hi, col_lo)
    scaled_ref[col] = own_row[...]
    for k in range(1, groups - 1):
        scaled_ref[col ^ k] = row_refs[k - 1][...] * occ_ref[col ^ k]
    scaled_ref[col ^ (groups - 1)] = jnp.zeros_like(own_row)
    left_hi[...], left_lo[...] = split(
        jnp.concatenate([scaled_ref[k] for k in range(groups)], axis=1)
    )


def early_kernel(groups, n_served, count, slots_ref, left_hi, left_lo, *refs):
    _, rest = two(count)
    chunk_refs, refs = refs[2 : 2 + len(rest)], refs[2 + len(rest) :]
    col_hi, col_lo, partial_ref, last_hi, last_lo = refs
    fill(lax.axis_index("row"), count, rest, chunk_refs, col_hi, col_lo)
    last = lax.axis_index("col") ^ (groups - 1)
    left = left_hi[...], left_lo[...]
    quarter = last_hi.shape[2]
    for i in range(n_served):
        right = tiles((col_hi, col_lo), slots_ref, i)
        partial_ref[i] = dot3(left, right)
        for out, side in zip((last_hi, last_lo), right):
            out[i] = pick(side, last, quarter)


def pick(x, index, size):
    out = x[:, :size]
    for k in range(1, x.shape[1] // size):
        out = jnp.where(index == k, x[:, k * size : (k + 1) * size], out)
    return out


def density_kernel(groups, row_ref, occ_ref, partial_ref, right_hi, right_lo, *outs):
    row_hi, row_lo = outs[:2]
    left = split(row_ref[...] * occ_ref[lax.axis_index("col") ^ (groups - 1)])
    row_hi[...], row_lo[...] = left
    for i, out in enumerate(outs[2:]):
        out[...] = partial_ref[i] + dot3(left, (right_hi[i], right_lo[i]))


def own_kernel(groups, phi_hi, phi_lo, strip_ref, left_hi, left_lo, row_hi, row_lo, *outs):
    out_ref, full_hi, full_lo = outs
    out_ref[...] = dot3((phi_hi[0], phi_lo[0]), split(strip_ref[...]))
    last = lax.axis_index("col") ^ (groups - 1)
    quarter = row_hi.shape[1]
    for full, left, row in ((full_hi, left_hi, row_hi), (full_lo, left_lo, row_lo)):
        full[...] = jnp.concatenate(
            [
                jnp.where(last == k, row[...], left[:, k * quarter : (k + 1) * quarter])
                for k in range(groups)
            ],
            axis=1,
        )


def strips_kernel(others, count, phi_hi, phi_lo, own_ref, *refs):
    strips, refs = refs[: len(others)], refs[len(others) :]
    first, _ = two(count)
    chunk_refs, (out_ref, col_hi, col_lo) = refs[: len(first)], refs[len(first) :]
    total = own_ref[...]
    for k, strip_ref in zip(others, strips):
        total += dot3((phi_hi[k], phi_lo[k]), split(strip_ref[...]))
    out_ref[...] = total
    fill(lax.axis_index("row"), count, first, chunk_refs, col_hi, col_lo)


def final_kernel(far, index, count, slots_ref, phi_hi, phi_lo, rows_ref, pot_ref, *refs):
    sum_ref, left_hi, left_lo = refs[:3]
    _, rest = two(count)
    chunk_refs, refs = refs[5 : 5 + len(rest)], refs[5 + len(rest) :]
    density_ref, potential_ref, col_hi, col_lo = refs
    fill(lax.axis_index("row"), count, rest, chunk_refs, col_hi, col_lo)
    strip = dot3((left_hi[...], left_lo[...]), tiles((col_hi, col_lo), slots_ref, index))
    coupled = sum_ref[...] + dot3((phi_hi[far], phi_lo[far]), split(strip))
    field = rows_ref[0] * coupled
    weights = pot_ref[...]
    parts = [field[:, at : at + TW] for at in range(0, field.shape[1], TW)]
    for at, part in enumerate(parts):
        potential_ref[:, at * TW : (at + 1) * TW] = jnp.sum(part * weights, axis=0, keepdims=True)
    ones = jnp.ones((8, TW), jnp.bfloat16)
    density_ref[...] = sum(
        lax.dot_general(ones, part, NT, preferred_element_type=jnp.float32)
        for part in split(sum(parts))
    )[:1]


def call(kernel, in_specs, outs, scratch=(), flops=0, aliases={}):
    out_specs = [SMEM if len(o.shape) == 1 else VMEM for o in outs]
    return pl.pallas_call(
        kernel,
        out_shape=outs,
        in_specs=in_specs,
        out_specs=out_specs,
        scratch_shapes=list(scratch),
        input_output_aliases=aliases,
        compiler_params=PARAMS,
        cost_estimate=pl.CostEstimate(flops=flops, bytes_accessed=2 << 20, transcendentals=0),
    )


def per_device(
    row_vectors,
    column_vectors,
    occupation,
    phi_row,
    phi_col,
    potential,
    tile_owner,
    tile_slot,
    correlation,
):
    groups = lax.axis_size("col")
    rows, quarter = row_vectors.shape
    states = occupation.shape[0]
    points = phi_col.shape[1]
    width = PAIR * TW
    block = column_vectors.shape[0] * lax.axis_size("row")
    far = groups // 2
    others = [k for k in range(groups - 1, 0, -1) if k != far]
    served = others + [0]
    f32 = lambda *shape: jax.ShapeDtypeStruct(shape, jnp.float32)
    bf16 = lambda *shape: jax.ShapeDtypeStruct(shape, jnp.bfloat16)
    row_pieces = gather_rows(row_vectors)
    chunks = gather_columns(column_vectors)
    far_chunks = gather_columns(flip(column_vectors, "col", far))
    n_served = len(served)
    in_hbm = lambda *arrays: [pltpu.with_memory_space_constraint(a, pltpu.HBM) for a in arrays]
    tables = [pltpu.SMEM(tile_owner.shape, jnp.int32)] * 2
    phi_hi, phi_lo, pot, rows_field = call(
        basis_kernel,
        [HBM] * 5,
        [bf16(groups, points, width)] * 2 + [f32(points, TW), f32(*phi_row.shape)],
        tables
        + [pltpu.VMEM(a.shape, jnp.float32) for a in (phi_col, potential)]
        + [pltpu.SemaphoreType.DMA((5,))],
    )(*in_hbm(tile_owner, correlation, phi_col, potential, phi_row))
    slots, occ, own_row, own_chunk = call(
        functools.partial(tables_kernel, served, far),
        [HBM] * 5,
        [
            jax.ShapeDtypeStruct(((n_served + 1) * PAIR,), jnp.int32),
            f32(groups, 1, quarter),
            f32(rows, quarter),
            f32(*column_vectors.shape),
        ],
        [
            pltpu.VMEM((rows, quarter), jnp.float32),
            *tables,
            pltpu.SemaphoreType.DMA((5,)),
        ],
    )(
        *in_hbm(
            tile_owner,
            tile_slot,
            occupation.reshape(groups, 1, quarter),
            row_vectors,
            column_vectors,
        )
    )
    count = len(chunks)
    first, rest = two(count)
    if count > 1:
        chunks[0] = own_chunk
    halves = [bf16(block, states)] * 2
    left_hi, left_lo, col_hi, col_lo = call(
        functools.partial(split_kernel, groups, count),
        [VMEM] * (groups + len(first)),
        [bf16(rows, states)] * 2 + halves,
        [pltpu.VMEM((groups, rows, quarter), jnp.float32)],
    )(occ, own_row, *row_pieces[1:-1], *(chunks[k] for k in first))
    _, _, partial, right_hi, right_lo = call(
        functools.partial(early_kernel, groups, n_served, count),
        [SMEM] + [VMEM] * (4 + len(rest)),
        [*halves, f32(n_served, rows, width), *[bf16(n_served, width, quarter)] * 2],
        (),
        6 * rows * width * states * n_served,
        {3: 0, 4: 1},
    )(slots, left_hi, left_lo, col_hi, col_lo, *(chunks[k] for k in rest))
    row_hi, row_lo, *strips = call(
        functools.partial(density_kernel, groups),
        [VMEM] * 5,
        [bf16(rows, quarter)] * 2 + [f32(rows, width)] * n_served,
        (),
        6 * rows * width * quarter * n_served,
    )(row_pieces[-1], occ, partial, right_hi, right_lo)
    strips = dict(zip(served, strips))
    arrived = [flip(strips[k], "col", k) for k in others]
    own, full_hi, full_lo = call(
        functools.partial(own_kernel, groups),
        [VMEM] * 7,
        [f32(points, rows)] + [bf16(rows, states)] * 2,
        (),
        6 * points * rows * width,
    )(phi_hi, phi_lo, strips[0], left_hi, left_lo, row_hi, row_lo)
    summed, far_hi, far_lo = call(
        functools.partial(strips_kernel, others, count),
        [VMEM] * (3 + len(others) + len(first)),
        [f32(points, rows), *halves],
        (),
        6 * points * rows * width * len(others),
    )(phi_hi, phi_lo, own, *arrived, *(far_chunks[k] for k in first))
    return tuple(
        call(
            functools.partial(final_kernel, far, n_served, count),
            [SMEM] + [VMEM] * (9 + len(rest)),
            [f32(1, points), f32(1, rows), *halves],
            (),
            0,
            {8: 2, 9: 3},
        )(
            *(slots, phi_hi, phi_lo, rows_field, pot, summed, full_hi, full_lo, far_hi, far_lo),
            *(far_chunks[k] for k in rest),
        )[:2]
    )


def solution(mesh):
    in_specs = (
        P("row", "col"),
        P(("col", "row"), None),
        P(),
        P(("row", "col"), None, None),
        P(("row", "col"), None, None),
        P(("row", "col"), None),
        P("row", None),
        P("row", None),
        P("row", None),
    )
    out_specs = (P(("row", "col"), None), P(("row", "col"), None))

    return jax.shard_map(
        per_device, mesh=mesh, in_specs=in_specs, out_specs=out_specs, check_vma=False
    )
```
